256 devices in a mesh: front: 16 (over z, core), row: 4 (over y), col: 4 (over x).
Axes of the slice: x: 4, y: 4, z: 8, core: 2. Of those that a mesh axis runs over, the one named last changes fastest.
Arguments:
- ancestor: bfloat16 [32768, 256], P('front'), may hold values from -6 to 6
- send_rows: int32 [16, 16, 4, 256], P('front', None, 'col'), may hold values from 0 to 2047, as said below
- send_count: int32 [16, 16, 4], P('front', None, 'col'), may hold values from 1 to 256, as said below
- border_coeff: bfloat16 [16, 4096, 16384], P('front', 'row', 'col'), may hold values from -0.0625 to 0.0625
- right_side: bfloat16 [16, 4096, 256], P('front', 'row'), may hold values from -6 to 6
- pivot_inverse: bfloat16 [16, 4096, 4096], P('front', 'row', 'col'), may hold values from -0.09375 to 0.09375
Outputs:
- solution: float32 [16, 256, 4096], P('front', 'row', 'col')
The draws below stay inside these ranges and needn't reach their ends.
Inputs may be any that keep to these rules, and one draw needn't show every extreme that they name: `send_rows`: row lists index the holder's own ancestor rows; entries past a slot's count are padding. `send_count`: loads differ from front to front; in every draw one front receives 256 rows from every holder in every column block.
All inputs are finite; a program needn't handle non-finite values.
Results may differ from the reference program's by a relative error of at most 0.015.
Values may be sent and summed in bfloat16 or wider, within the bound.
No kernel may reach another device: no remote copies, remote signals or barrier semaphores. Data moves between devices by JAX's collectives and lax.ppermute only.
A program may use at most 64 MiB of HBM per device.

```python
import jax
import jax.numpy as jnp
from jax import lax

NP = 4096
S = 256
ANC_DEV = 2048
FRONTS = 16
COLS = 4
CAP = 256
BORDER = 16384
ANC = 32768
N_ROW = 4
N_COL = 4


def draw_send_rows(key, part):
    rows = jax.random.randint(jax.random.fold_in(key, 11), (FRONTS, FRONTS, COLS, CAP), 0, ANC_DEV, dtype=jnp.int32)
    flat = rows.reshape(-1)
    flat = flat.at[0].set(ANC_DEV - 1)
    flat = flat.at[1].set(0)
    return flat.reshape(FRONTS, FRONTS, COLS, CAP)


def draw_send_count(key, part):
    level = jax.random.randint(jax.random.fold_in(key, 21), (FRONTS,), 1, 5, dtype=jnp.int32)
    minus = jax.random.randint(jax.random.fold_in(key, 22), (FRONTS, FRONTS, COLS), 0, CAP // 4 + 1, dtype=jnp.int32)
    counts = jnp.maximum(1, level[None, :, None] * CAP // 4 - minus)
    counts = jnp.minimum(counts, CAP)
    full_front = jax.random.randint(jax.random.fold_in(key, 23), (), 0, FRONTS, dtype=jnp.int32)
    fronts = jnp.arange(FRONTS, dtype=jnp.int32)
    counts = jnp.where((fronts == full_front)[None, :, None], CAP, counts)
    low_front = (full_front + 1) % FRONTS
    low_holder = jax.random.randint(jax.random.fold_in(key, 24), (), 0, FRONTS, dtype=jnp.int32)
    pair = (fronts[:, None, None] == low_holder) & (fronts[None, :, None] == low_front)
    hit = jnp.broadcast_to(pair, (FRONTS, FRONTS, COLS))
    single = jnp.where(hit & (low_front != full_front), 1, counts)
    return single.astype(jnp.int32)


def steps_of(own_key, extent, cuts, least, high):
    gain, own = 1.0, jax.random.fold_in(own_key, 6)
    for axis_at, parts in cuts:
        steps = jnp.exp(jax.random.uniform(jax.random.fold_in(own, axis_at), (parts,), jnp.float32, least / len(cuts), high / len(cuts)))
        gain = gain * jnp.repeat(steps, extent[axis_at] // parts).reshape([-1 if axis == axis_at else 1 for axis in range(len(extent))])
    return gain


def centred(key, dims, spread, reach, split=(), held_as=jnp.bfloat16):
    array = spread * jax.random.normal(key, dims, jnp.float32)
    if split:
        array = array * steps_of(key, dims, split, -0.22, 0.18)
    return jnp.clip(array, -reach, reach).astype(held_as)


def setup_inputs(seed: int = 0) -> dict:
    seeds = jax.random.split(jax.random.key(seed), 7)
    ancestor = centred(seeds[0], (ANC, S), 1.0, 6.0, ((0, 16),))
    send_rows = draw_send_rows(jax.random.fold_in(seeds[6], 71), 0)
    send_count = draw_send_count(jax.random.fold_in(seeds[6], 71), 0)
    border_coeff = centred(seeds[3], (FRONTS, NP, BORDER), (BORDER // 2) ** -0.5, 0.0625, ((0, 16), (1, 4), (2, 4)))
    right_side = centred(seeds[4], (FRONTS, NP, S), 1.0, 6.0, ((0, 16), (1, 4)))
    pivot_inverse = centred(seeds[5], (FRONTS, NP, NP), NP ** -0.5, 0.09375, ((0, 16), (1, 4), (2, 4)))
    return dict(ancestor=ancestor, send_rows=send_rows, send_count=send_count, border_coeff=border_coeff, right_side=right_side, pivot_inverse=pivot_inverse)


def reference(ancestor, send_rows, send_count, border_coeff, right_side, pivot_inverse):
    held = ancestor.reshape(FRONTS, ANC_DEV, S)
    holders = jnp.arange(FRONTS, dtype=jnp.int32)
    positions = jnp.arange(CAP, dtype=jnp.int32)
    col_width = FRONTS * CAP
    row_width = NP // N_ROW

    def one_front(inputs):
        front_id, coeff, rhs, inverse = inputs
        rows_d = send_rows[:, front_id].astype(jnp.int32)
        counts_d = send_count[:, front_id]
        picked = held[holders[:, None, None], rows_d]
        alive = positions[None, None, :] < counts_d[:, :, None]
        picked = jnp.where(alive[..., None], picked, jnp.zeros_like(picked))
        border = jnp.transpose(picked, (1, 0, 2, 3)).reshape(N_COL, col_width, S)
        total = jnp.zeros((NP, S), jnp.float32)
        for block in range(N_COL):
            part = jnp.dot(coeff[:, block * col_width:(block + 1) * col_width], border[block],
                           preferred_element_type=jnp.float32)
            total = total + part.astype(jnp.bfloat16).astype(jnp.float32)
        residual = (rhs.astype(jnp.float32) - total).astype(jnp.bfloat16)
        answer = jnp.zeros((S, NP), jnp.float32)
        for block in range(N_ROW):
            term = jnp.dot(residual[block * row_width:(block + 1) * row_width].T,
                           inverse[block * row_width:(block + 1) * row_width],
                           preferred_element_type=jnp.float32)
            answer = answer + term.astype(jnp.bfloat16).astype(jnp.float32)
        return answer

    return lax.map(one_front, (holders, border_coeff, right_side, pivot_inverse))
```

```python
import jax
import jax.numpy as jnp
from jax import lax
from jax.experimental import pallas as pl
from jax.experimental.pallas import tpu as pltpu
from jax.sharding import PartitionSpec as P


def shifted(shard, axis, step):
    peers = lax.axis_size(axis)
    return lax.ppermute(shard, axis, [(i, (i + step) % peers) for i in range(peers)])


def even_swap(shard, axis):
    peers = lax.axis_size(axis)
    return lax.ppermute(shard, axis, [(i, i ^ 1) for i in range(peers)])


def odd_swap(shard, axis):
    peers = lax.axis_size(axis)
    return lax.ppermute(shard, axis, [(i, (i + (1 if i % 2 else -1)) % peers) for i in range(peers)])


def pick_kernel(counts_ref, lists_ref, ancestor_ref, out_ref):
    fronts, slot_rows = lists_ref.shape
    held = ancestor_ref.shape[0]
    share = slot_rows // lax.axis_size("row")
    first = lax.axis_index("row") * share
    lists = pltpu.roll(lists_ref[...], lax.rem(slot_rows - first, slot_rows), 1)
    lane = lax.broadcasted_iota(jnp.int32, lists.shape, 1)
    line = lax.broadcasted_iota(jnp.int32, lists.shape, 0)
    limit = jnp.zeros_like(lists)
    for d in range(fronts):
        limit = jnp.where(line == d, counts_ref[d], limit)
    lists = jnp.where(lane + first < limit, lists, -1)
    partner = pltpu.roll(pltpu.roll(lists, share, 1), fronts - 1, 0)
    pairs = jnp.where(lane < share, lists, partner)[:, : 2 * share]
    ancestor = ancestor_ref[...]
    row = lax.broadcasted_iota(jnp.int32, (held, 2 * share), 0)
    for p in range(fronts // 2):
        chosen = (row == pairs[2 * p : 2 * p + 1, :]).astype(jnp.bfloat16)
        picked = lax.dot_general(
            chosen, ancestor, (((0,), (0,)), ((), ())), preferred_element_type=jnp.float32
        )
        out_ref[pl.ds(2 * p * share, 2 * share), :] = picked.astype(jnp.bfloat16)


def pick_rows(ancestor, lists, counts):
    fronts, slot_rows = lists.shape
    share = slot_rows // lax.axis_size("row")
    vmem = pl.BlockSpec(memory_space=pltpu.VMEM)
    picked = pl.pallas_call(
        pick_kernel,
        out_shape=jax.ShapeDtypeStruct((fronts * share, ancestor.shape[1]), jnp.bfloat16),
        in_specs=[pl.BlockSpec(memory_space=pltpu.SMEM), vmem, vmem],
        out_specs=vmem,
    )(counts, lists, ancestor)
    return picked.reshape(fronts, share, ancestor.shape[1])


def gathered_along_row(shard):
    fronts, share, sources = shard.shape
    half = fronts // 2
    me = lax.axis_index("row")
    peers = lax.axis_size("row")
    before = shifted(shard, "row", 1)
    after = shifted(shard, "row", -1)
    low = shifted(before[:half], "row", 1)
    high = shifted(after[half:], "row", -1)
    border = jnp.zeros((fronts, peers, share, sources), shard.dtype)
    for tile, start, step in (
        (shard, 0, 0),
        (before, 0, peers - 1),
        (after, 0, 1),
        (low, 0, 2),
        (high, half, 2),
    ):
        where = lax.rem(me + step, peers)
        border = lax.dynamic_update_slice(border, tile[:, None], (start, where, 0, 0))
    return border.reshape(fronts * peers * share, sources)


def added(a, b):
    return (a.astype(jnp.float32) + b.astype(jnp.float32)).astype(jnp.bfloat16)


def per_device(ancestor, send_rows, send_count, border_coeff, right_side, pivot_inverse):
    outgoing = pick_rows(ancestor, send_rows[0, :, 0, :], send_count[0, :, 0])
    arrived = lax.all_to_all(outgoing, "front", split_axis=0, concat_axis=0, tiled=True)
    border = gathered_along_row(arrived)
    coeff = border_coeff[0]
    rhs = right_side[0]
    inverse = pivot_inverse[0]
    half = coeff.shape[0] // 2
    parts = []
    for i, (one, two) in enumerate(((even_swap, odd_swap), (odd_swap, even_swap))):
        rows = slice(i * half, (i + 1) * half)
        part = jnp.dot(coeff[rows], border, preferred_element_type=jnp.float32).astype(jnp.bfloat16)
        pair = added(part, one(part, "col"))
        other = two(pair, "col")
        total = pair.astype(jnp.float32) + other.astype(jnp.float32)
        parts.append((rhs[rows].astype(jnp.float32) - total).astype(jnp.bfloat16))
    residual = jnp.concatenate(parts, 0)
    term = lax.dot_general(
        residual, inverse, (((0,), (0,)), ((), ())), preferred_element_type=jnp.float32
    ).astype(jnp.bfloat16)
    peers = lax.axis_size("row")
    tiles = term.reshape(peers, term.shape[0] // peers, term.shape[1])
    tiles = lax.all_to_all(tiles, "row", 0, 0, tiled=True)
    return jnp.sum(tiles.astype(jnp.float32), axis=0)[None]


def solution(mesh):
    return jax.shard_map(
        per_device,
        mesh=mesh,
        in_specs=(
            P("front", None),
            P("front", None, "col", None),
            P("front", None, "col"),
            P("front", "row", "col"),
            P("front", "row", None),
            P("front", "row", "col"),
        ),
        out_specs=P("front", "row", "col"),
        check_vma=False,
    )
```

```python
import functools

import jax
import jax.numpy as jnp
from jax import lax
from jax.experimental import pallas as pl
from jax.experimental.pallas import tpu as pltpu
from jax.sharding import PartitionSpec as P


def shifted(shard, axis, step):
    peers = lax.axis_size(axis)
    return lax.ppermute(shard, axis, [(i, (i + step) % peers) for i in range(peers)])


def even_swap(shard, axis):
    peers = lax.axis_size(axis)
    return lax.ppermute(shard, axis, [(i, i ^ 1) for i in range(peers)])


def odd_swap(shard, axis):
    peers = lax.axis_size(axis)
    return lax.ppermute(shard, axis, [(i, (i + (1 if i % 2 else -1)) % peers) for i in range(peers)])


FAR = (4, 3, -3)
MID = (2, -2)
NEAR = (1, -1, 0)
CHIPS = 8


def along_chips(shard, step):
    peers = lax.axis_size("front")
    return lax.ppermute(shard, "front", [(i, (i + 2 * step) % peers) for i in range(peers)])


def place():
    front = lax.axis_index("front")
    return lax.shift_right_logical(front, 1), lax.bitwise_and(front, 1)


def picked_rows(ancestor, index):
    row = lax.broadcasted_iota(jnp.int32, (ancestor.shape[0], index.shape[1]), 0)
    chosen = (row == index).astype(jnp.bfloat16)
    return lax.dot_general(
        chosen, ancestor, (((0,), (0,)), ((), ())), preferred_element_type=jnp.float32
    ).astype(jnp.bfloat16)


def pick_shares_kernel(
    counts_hbm, lists_hbm, ancestor_hbm, kept_ref, sent_ref, live_ref, held_ref, counts_ref, sems
):
    copies = [
        pltpu.make_async_copy(source, target, sems.at[i])
        for i, (source, target) in enumerate(
            ((counts_hbm, counts_ref), (lists_hbm.at[0], live_ref), (ancestor_hbm, held_ref))
        )
    ]
    for copy in copies:
        copy.start()
    for copy in copies[:2]:
        copy.wait()
    slot_rows = live_ref.shape[-1]
    share = slot_rows // lax.axis_size("row")
    first = lax.axis_index("row") * share
    chip, core = place()
    lane = lax.broadcasted_iota(jnp.int32, (1, 2 * share), 1)
    slot = lax.broadcasted_iota(jnp.int32, (1, slot_rows), 1)
    for d in range(live_ref.shape[0]):
        live_ref[d] = jnp.where(slot < counts_ref[d], live_ref[d], -1)

    def rolled(d, start):
        row = jnp.broadcast_to(live_ref[d], (8, slot_rows))
        return pltpu.roll(row, lax.rem(slot_rows - first + start, slot_rows), 1)[:1, : 2 * share]

    chosen = []
    for step in FAR:
        target = 2 * lax.rem(chip + step + CHIPS, CHIPS)
        kept, sent = rolled(target + core, 0), rolled(target + 1 - core, share)
        chosen.append(jnp.where(lane < share, kept, sent))
    copies[2].wait()
    for i, index in enumerate(chosen):
        rows = picked_rows(held_ref[...], index)
        kept_ref[i] = rows[:share]
        sent_ref[i] = rows[share:]


def pick_slots_kernel(steps, live_ref, held_ref, kept_ref, sent_ref):
    chip, core = place()
    ancestor = held_ref[...]
    for i, step in enumerate(steps):
        target = 2 * lax.rem(chip + step + CHIPS, CHIPS)
        for d, ref in ((target + 1 - core, sent_ref), (target + core, kept_ref)):
            ref[i] = picked_rows(ancestor, live_ref[d])


def pick_shares(counts, lists, ancestor):
    share = lists.shape[-1] // lax.axis_size("row")
    vmem = pl.BlockSpec(memory_space=pltpu.VMEM)
    shape = jax.ShapeDtypeStruct((len(FAR), share, ancestor.shape[1]), ancestor.dtype)
    return pl.pallas_call(
        pick_shares_kernel,
        out_shape=(
            shape,
            shape,
            jax.ShapeDtypeStruct(lists.shape[1:], lists.dtype),
            jax.ShapeDtypeStruct(ancestor.shape, ancestor.dtype),
        ),
        in_specs=[pl.BlockSpec(memory_space=pltpu.HBM)] * 3,
        out_specs=(vmem,) * 4,
        scratch_shapes=[
            pltpu.SMEM(counts.shape, counts.dtype),
            pltpu.SemaphoreType.DMA((3,)),
        ],
        compiler_params=pltpu.CompilerParams(vmem_limit_bytes=24 << 20),
    )(*(pltpu.with_memory_space_constraint(x, pltpu.HBM) for x in (counts, lists, ancestor)))


def pick_slots(steps, lists, ancestor):
    vmem = pl.BlockSpec(memory_space=pltpu.VMEM)
    rows = lists.shape[-1]
    shape = jax.ShapeDtypeStruct((len(steps), rows, ancestor.shape[1]), ancestor.dtype)
    return pl.pallas_call(
        functools.partial(pick_slots_kernel, steps),
        out_shape=(shape, shape),
        in_specs=[vmem, vmem],
        out_specs=(vmem, vmem),
        compiler_params=pltpu.CompilerParams(vmem_limit_bytes=24 << 20),
        cost_estimate=pl.CostEstimate(
            flops=4 * len(steps) * rows * ancestor.size,
            bytes_accessed=2 * ancestor.size,
            transcendentals=0,
        ),
    )(lists, ancestor)


def columns(coeff_ref, chip, top, height):
    width = coeff_ref.shape[1] // CHIPS
    return coeff_ref[top : top + height, pl.ds(pl.multiple_of(chip * width, width), width)]


def near_kernel(coeff_ref, kept_ref, came_ref, *refs):
    *part_refs, sum_ref, rows_ref = refs
    chip, core = place()
    slot_rows = kept_ref.shape[0]
    kept, came = kept_ref[...], came_ref[...]
    rows_ref[0, :slot_rows] = jnp.where(core == 0, kept, came)
    rows_ref[0, slot_rows:] = jnp.where(core == 0, came, kept)
    pivots = coeff_ref.shape[0]
    sum_ref[...] = jnp.dot(
        columns(coeff_ref, chip, 0, pivots), rows_ref[0], preferred_element_type=jnp.float32
    )
    for i, (step, part_ref) in enumerate(zip(MID + NEAR[:2], part_refs, strict=True), 1):
        for holder in range(2):
            rows_ref[i, holder * slot_rows : (holder + 1) * slot_rows] = part_ref[
                lax.bitwise_xor(core, holder)
            ]
        sum_ref[...] += jnp.dot(
            columns(coeff_ref, lax.rem(chip - step + CHIPS, CHIPS), 0, pivots),
            rows_ref[i],
            preferred_element_type=jnp.float32,
        )


def far_kernel(
    part, coeff_ref, sum_ref, own_ref, across_ref, before_ref, after_ref, out_ref, rows_ref
):
    chip, core = place()
    me = lax.axis_index("row")
    peers = lax.axis_size("row")
    share = own_ref.shape[2]
    half = out_ref.shape[0]
    total = sum_ref[part * half : (part + 1) * half]
    for i, step in enumerate(FAR):
        for block in range(peers):
            back = lax.rem(block - me + peers, peers)
            for holder in range(2):
                piece = before_ref[i, lax.bitwise_xor(core, holder)]
                for away, part_ref in ((2, across_ref), (1, after_ref), (0, own_ref)):
                    piece = jnp.where(
                        back == away, part_ref[i, lax.bitwise_xor(core, holder)], piece
                    )
                start = (holder * peers + block) * share
                rows_ref[i, start : start + share, :] = piece
        total = total + jnp.dot(
            columns(coeff_ref, lax.rem(chip - step + CHIPS, CHIPS), part * half, half),
            rows_ref[i],
            preferred_element_type=jnp.float32,
        )
    out_ref[...] = total.astype(out_ref.dtype)


def products(coeff, kept, came, mid, near, shares):
    vmem = pl.BlockSpec(memory_space=pltpu.VMEM)
    pivots, sources = coeff.shape[0], kept.shape[-1]
    depth = coeff.shape[1] // CHIPS

    def cost(blocks):
        return pl.CostEstimate(
            flops=int(2 * blocks) * depth * pivots * sources,
            bytes_accessed=int(2 * blocks) * depth * (pivots + sources),
            transcendentals=0,
        )

    total = pl.pallas_call(
        near_kernel,
        out_shape=jax.ShapeDtypeStruct((pivots, sources), jnp.float32),
        in_specs=[vmem] * 7,
        out_specs=vmem,
        scratch_shapes=[pltpu.VMEM((len(MID + NEAR), depth, sources), coeff.dtype)],
        compiler_params=pltpu.CompilerParams(vmem_limit_bytes=24 << 20),
        cost_estimate=cost(5),
    )(coeff, kept, came, *mid, *near)
    half = jax.ShapeDtypeStruct((pivots // 2, sources), coeff.dtype)
    return [
        pl.pallas_call(
            functools.partial(far_kernel, part),
            out_shape=half,
            in_specs=[vmem] * 6,
            out_specs=vmem,
            scratch_shapes=[pltpu.VMEM((len(FAR), depth, sources), coeff.dtype)],
            compiler_params=pltpu.CompilerParams(vmem_limit_bytes=24 << 20),
            cost_estimate=cost(len(FAR) / 2),
        )(coeff, total, *shares)
        for part in range(2)
    ]


def added(a, b):
    return (a.astype(jnp.float32) + b.astype(jnp.float32)).astype(jnp.bfloat16)


def per_device(ancestor, send_rows, send_count, border_coeff, right_side, pivot_inverse):
    kept, sent, live, held = pick_shares(send_count.reshape(-1), send_rows, ancestor)
    came = even_swap(sent, "front")
    far = jnp.stack([kept, came], 1)
    kept, sent = pick_slots(NEAR, live, held)
    came = even_swap(sent, "front")
    near = jnp.stack([kept, came], 1)
    kept, sent = pick_slots(MID, live, held)
    came = even_swap(sent, "front")
    mid = jnp.stack([kept, came], 1)
    sent = []
    for part, steps in ((near, NEAR[:2]), (far, FAR), (mid, MID)):
        for i, step in enumerate(steps):
            sent.append(along_chips(part[i], step))
    near_parts, shares, mid_parts = sent[:2], jnp.stack(sent[2:5]), sent[5:]
    shares = [shares]
    for step in (2, 1, -1):
        shares.append(shifted(shares[0], "row", step))
    coeff = pltpu.with_memory_space_constraint(border_coeff[0], pltpu.VMEM)
    rhs = right_side[0]
    inverse = pivot_inverse[0]
    half = coeff.shape[0] // 2
    halves = products(coeff, near[2, 0], near[2, 1], mid_parts, near_parts, shares)
    parts = []
    for i, (one, two) in enumerate(((even_swap, odd_swap), (odd_swap, even_swap))):
        rows = slice(i * half, (i + 1) * half)
        pair = added(halves[i], one(halves[i], "col"))
        other = two(pair, "col")
        total = pair.astype(jnp.float32) + other.astype(jnp.float32)
        parts.append((rhs[rows].astype(jnp.float32) - total).astype(jnp.bfloat16))
    residual = jnp.concatenate(parts, 0)
    term = lax.dot_general(
        residual, inverse, (((0,), (0,)), ((), ())), preferred_element_type=jnp.float32
    ).astype(jnp.bfloat16)
    peers = lax.axis_size("row")
    tiles = term.reshape(peers, term.shape[0] // peers, term.shape[1])
    tiles = lax.all_to_all(tiles, "row", 0, 0, tiled=True)
    return jnp.sum(tiles.astype(jnp.float32), axis=0)[None]


def solution(mesh):
    return sharded(per_device, mesh)


def sharded(body, mesh):
    return jax.shard_map(
        body,
        mesh=mesh,
        in_specs=(
            P("front", None),
            P("front", None, "col", None),
            P("front", None, "col"),
            P("front", "row", "col"),
            P("front", "row", None),
            P("front", "row", "col"),
        ),
        out_specs=P("front", "row", "col"),
        check_vma=False,
    )
```

```python
import functools

import jax
import jax.numpy as jnp
from jax import lax
from jax.experimental import pallas as pl
from jax.experimental.pallas import tpu as pltpu
from jax.sharding import PartitionSpec as P


def shifted(shard, axis, step):
    peers = lax.axis_size(axis)
    return lax.ppermute(shard, axis, [(i, (i + step) % peers) for i in range(peers)])


def even_swap(shard, axis):
    peers = lax.axis_size(axis)
    return lax.ppermute(shard, axis, [(i, i ^ 1) for i in range(peers)])


def odd_swap(shard, axis):
    peers = lax.axis_size(axis)
    return lax.ppermute(shard, axis, [(i, (i + (1 if i % 2 else -1)) % peers) for i in range(peers)])


FAR = ((4, 4), (3, 3), (-3, -3), (-2, 2))
MID = ((2, -2),)
NEAR = ((1, 1), (-1, -1), (0, 0))
CHIPS = 8


def along_chips(shard, step):
    peers = lax.axis_size("front")
    return lax.ppermute(shard, "front", [(i, (i + 2 * step[i % 2]) % peers) for i in range(peers)])


def moved(chip, step, core, sign):
    here = step[0] + core * (step[1] - step[0])
    return lax.rem(chip + sign * here + CHIPS, CHIPS)


def place():
    front = lax.axis_index("front")
    return lax.shift_right_logical(front, 1), lax.bitwise_and(front, 1)


def picked_rows(ancestor, index):
    row = lax.broadcasted_iota(jnp.int32, (ancestor.shape[0], index.shape[1]), 0)
    chosen = (row == index).astype(jnp.bfloat16)
    return lax.dot_general(
        chosen, ancestor, (((0,), (0,)), ((), ())), preferred_element_type=jnp.float32
    ).astype(jnp.bfloat16)


def pick_shares_kernel(
    counts_hbm, lists_hbm, ancestor_hbm, kept_ref, sent_ref, live_ref, held_ref, counts_ref, sems
):
    copies = [
        pltpu.make_async_copy(source, target, sems.at[i])
        for i, (source, target) in enumerate(
            ((counts_hbm, counts_ref), (lists_hbm.at[0], live_ref), (ancestor_hbm, held_ref))
        )
    ]
    for copy in copies:
        copy.start()
    for copy in copies[:2]:
        copy.wait()
    slot_rows = live_ref.shape[-1]
    share = slot_rows // lax.axis_size("row")
    first = lax.axis_index("row") * share
    chip, core = place()
    lane = lax.broadcasted_iota(jnp.int32, (1, 2 * share), 1)
    slot = lax.broadcasted_iota(jnp.int32, (1, slot_rows), 1)
    for d in range(live_ref.shape[0]):
        live_ref[d] = jnp.where(slot < counts_ref[d], live_ref[d], -1)

    def rolled(d, start):
        row = jnp.broadcast_to(live_ref[d], (8, slot_rows))
        return pltpu.roll(row, lax.rem(slot_rows - first + start, slot_rows), 1)[:1, : 2 * share]

    chosen = []
    for step in FAR:
        kept = rolled(2 * moved(chip, step, core, 1) + core, 0)
        sent = rolled(2 * moved(chip, step, 1 - core, 1) + 1 - core, share)
        chosen.append(jnp.where(lane < share, kept, sent))
    copies[2].wait()
    for i, index in enumerate(chosen):
        rows = picked_rows(held_ref[...], index)
        kept_ref[i] = rows[:share]
        sent_ref[i] = rows[share:]


def pick_slots_kernel(steps, live_ref, held_ref, kept_ref, sent_ref):
    chip, core = place()
    ancestor = held_ref[...]
    for i, step in enumerate(steps):
        for to, ref in ((1 - core, sent_ref), (core, kept_ref)):
            ref[i] = picked_rows(ancestor, live_ref[2 * moved(chip, step, to, 1) + to])


def pick_shares(counts, lists, ancestor):
    share = lists.shape[-1] // lax.axis_size("row")
    vmem = pl.BlockSpec(memory_space=pltpu.VMEM)
    shape = jax.ShapeDtypeStruct((len(FAR), share, ancestor.shape[1]), ancestor.dtype)
    return pl.pallas_call(
        pick_shares_kernel,
        out_shape=(
            shape,
            shape,
            jax.ShapeDtypeStruct(lists.shape[1:], lists.dtype),
            jax.ShapeDtypeStruct(ancestor.shape, ancestor.dtype),
        ),
        in_specs=[pl.BlockSpec(memory_space=pltpu.HBM)] * 3,
        out_specs=(vmem,) * 4,
        scratch_shapes=[
            pltpu.SMEM(counts.shape, counts.dtype),
            pltpu.SemaphoreType.DMA((3,)),
        ],
        compiler_params=pltpu.CompilerParams(vmem_limit_bytes=24 << 20),
    )(*(pltpu.with_memory_space_constraint(x, pltpu.HBM) for x in (counts, lists, ancestor)))


def pick_slots(steps, lists, ancestor):
    vmem = pl.BlockSpec(memory_space=pltpu.VMEM)
    rows = lists.shape[-1]
    shape = jax.ShapeDtypeStruct((len(steps), rows, ancestor.shape[1]), ancestor.dtype)
    return pl.pallas_call(
        functools.partial(pick_slots_kernel, steps),
        out_shape=(shape, shape),
        in_specs=[vmem, vmem],
        out_specs=(vmem, vmem),
        compiler_params=pltpu.CompilerParams(vmem_limit_bytes=24 << 20),
        cost_estimate=pl.CostEstimate(
            flops=4 * len(steps) * rows * ancestor.size,
            bytes_accessed=2 * ancestor.size,
            transcendentals=0,
        ),
    )(lists, ancestor)


def columns(coeff_ref, chip, top, height):
    width = coeff_ref.shape[1] // CHIPS
    return coeff_ref[top : top + height, pl.ds(pl.multiple_of(chip * width, width), width)]


def near_kernel(coeff_ref, kept_ref, came_ref, *refs):
    *part_refs, sum_ref, rows_ref = refs
    chip, core = place()
    slot_rows = kept_ref.shape[0]
    kept, came = kept_ref[...], came_ref[...]
    rows_ref[0, :slot_rows] = jnp.where(core == 0, kept, came)
    rows_ref[0, slot_rows:] = jnp.where(core == 0, came, kept)
    pivots = coeff_ref.shape[0]
    sum_ref[...] = jnp.dot(
        columns(coeff_ref, chip, 0, pivots), rows_ref[0], preferred_element_type=jnp.float32
    )
    for i, (step, part_ref) in enumerate(zip(MID + NEAR[:2], part_refs, strict=True), 1):
        for holder in range(2):
            rows_ref[i, holder * slot_rows : (holder + 1) * slot_rows] = part_ref[
                lax.bitwise_xor(core, holder)
            ]
        sum_ref[...] += jnp.dot(
            columns(coeff_ref, moved(chip, step, core, -1), 0, pivots),
            rows_ref[i],
            preferred_element_type=jnp.float32,
        )


def far_kernel(
    part, coeff_ref, sum_ref, own_ref, across_ref, before_ref, after_ref, out_ref, rows_ref
):
    chip, core = place()
    me = lax.axis_index("row")
    peers = lax.axis_size("row")
    share = own_ref.shape[2]
    half = out_ref.shape[0]
    total = sum_ref[part * half : (part + 1) * half]
    for i, step in enumerate(FAR):
        for block in range(peers):
            back = lax.rem(block - me + peers, peers)
            for holder in range(2):
                piece = before_ref[i, lax.bitwise_xor(core, holder)]
                for away, part_ref in ((2, across_ref), (1, after_ref), (0, own_ref)):
                    piece = jnp.where(
                        back == away, part_ref[i, lax.bitwise_xor(core, holder)], piece
                    )
                start = (holder * peers + block) * share
                rows_ref[i, start : start + share, :] = piece
        total = total + jnp.dot(
            columns(coeff_ref, moved(chip, step, core, -1), part * half, half),
            rows_ref[i],
            preferred_element_type=jnp.float32,
        )
    out_ref[...] = total.astype(out_ref.dtype)


def products(coeff, kept, came, mid, near, shares):
    vmem = pl.BlockSpec(memory_space=pltpu.VMEM)
    pivots, sources = coeff.shape[0], kept.shape[-1]
    depth = coeff.shape[1] // CHIPS

    def cost(blocks):
        return pl.CostEstimate(
            flops=int(2 * blocks) * depth * pivots * sources,
            bytes_accessed=int(2 * blocks) * depth * (pivots + sources),
            transcendentals=0,
        )

    total = pl.pallas_call(
        near_kernel,
        out_shape=jax.ShapeDtypeStruct((pivots, sources), jnp.float32),
        in_specs=[vmem] * (len(MID + NEAR) + 2),
        out_specs=vmem,
        scratch_shapes=[pltpu.VMEM((len(MID + NEAR), depth, sources), coeff.dtype)],
        compiler_params=pltpu.CompilerParams(vmem_limit_bytes=24 << 20),
        cost_estimate=cost(len(MID + NEAR)),
    )(coeff, kept, came, *mid, *near)
    half = jax.ShapeDtypeStruct((pivots // 2, sources), coeff.dtype)
    return [
        pl.pallas_call(
            functools.partial(far_kernel, part),
            out_shape=half,
            in_specs=[vmem] * 6,
            out_specs=vmem,
            scratch_shapes=[pltpu.VMEM((len(FAR), depth, sources), coeff.dtype)],
            compiler_params=pltpu.CompilerParams(vmem_limit_bytes=24 << 20),
            cost_estimate=cost(len(FAR) / 2),
        )(coeff, total, *shares)
        for part in range(2)
    ]


def added(a, b):
    return (a.astype(jnp.float32) + b.astype(jnp.float32)).astype(jnp.bfloat16)


def per_device(ancestor, send_rows, send_count, border_coeff, right_side, pivot_inverse):
    kept, sent, live, held = pick_shares(send_count.reshape(-1), send_rows, ancestor)
    came = even_swap(sent, "front")
    far = jnp.stack([kept, came], 1)
    kept, sent = pick_slots(NEAR, live, held)
    came = even_swap(sent, "front")
    near = jnp.stack([kept, came], 1)
    kept, sent = pick_slots(MID, live, held)
    came = even_swap(sent, "front")
    mid = jnp.stack([kept, came], 1)
    sent = []
    for part, steps in ((near, NEAR[:2]), (far, FAR), (mid, MID)):
        for i, step in enumerate(steps):
            sent.append(along_chips(part[i], step))
    near_parts, mid_parts = sent[:2], sent[2 + len(FAR) :]
    shares = [jnp.stack(sent[2 : 2 + len(FAR)])]
    for step in (2, 1, -1):
        shares.append(shifted(shares[0], "row", step))
    coeff = pltpu.with_memory_space_constraint(border_coeff[0], pltpu.VMEM)
    rhs = right_side[0]
    inverse = pivot_inverse[0]
    half = coeff.shape[0] // 2
    halves = products(coeff, near[2, 0], near[2, 1], mid_parts, near_parts, shares)
    parts = []
    for i, (one, two) in enumerate(((even_swap, odd_swap), (odd_swap, even_swap))):
        rows = slice(i * half, (i + 1) * half)
        pair = added(halves[i], one(halves[i], "col"))
        other = two(pair, "col")
        total = pair.astype(jnp.float32) + other.astype(jnp.float32)
        parts.append((rhs[rows].astype(jnp.float32) - total).astype(jnp.bfloat16))
    residual = jnp.concatenate(parts, 0)
    term = lax.dot_general(
        residual, inverse, (((0,), (0,)), ((), ())), preferred_element_type=jnp.float32
    ).astype(jnp.bfloat16)
    peers = lax.axis_size("row")
    tiles = term.reshape(peers, term.shape[0] // peers, term.shape[1])
    tiles = lax.all_to_all(tiles, "row", 0, 0, tiled=True)
    return jnp.sum(tiles.astype(jnp.float32), axis=0)[None]


def solution(mesh):
    return sharded(per_device, mesh)


def sharded(body, mesh):
    return jax.shard_map(
        body,
        mesh=mesh,
        in_specs=(
            P("front", None),
            P("front", None, "col", None),
            P("front", None, "col"),
            P("front", "row", "col"),
            P("front", "row", None),
            P("front", "row", "col"),
        ),
        out_specs=P("front", "row", "col"),
        check_vma=False,
    )
```

```python
import functools

import jax
import jax.numpy as jnp
from jax import lax
from jax.experimental import pallas as pl
from jax.experimental.pallas import tpu as pltpu
from jax.sharding import PartitionSpec as P


def shifted(shard, axis, step):
    peers = lax.axis_size(axis)
    return lax.ppermute(shard, axis, [(i, (i + step) % peers) for i in range(peers)])


def even_swap(shard, axis):
    peers = lax.axis_size(axis)
    return lax.ppermute(shard, axis, [(i, i ^ 1) for i in range(peers)])


def odd_swap(shard, axis):
    peers = lax.axis_size(axis)
    return lax.ppermute(shard, axis, [(i, (i + (1 if i % 2 else -1)) % peers) for i in range(peers)])


FAR = ((4, 4), (3, 3), (-3, -3), (-2, 2))
MID = ((2, -2),)
NEAR = ((1, 1), (-1, -1), (0, 0))
CHIPS = 8


def along_chips(shard, step):
    peers = lax.axis_size("front")
    return lax.ppermute(shard, "front", [(i, (i + 2 * step[i % 2]) % peers) for i in range(peers)])


def moved(chip, step, core, sign):
    here = step[0] + core * (step[1] - step[0])
    return lax.rem(chip + sign * here + CHIPS, CHIPS)


def place():
    front = lax.axis_index("front")
    return lax.shift_right_logical(front, 1), lax.bitwise_and(front, 1)


def picked_rows(ancestor, index):
    row = lax.broadcasted_iota(jnp.int32, (ancestor.shape[0], index.shape[1]), 0)
    chosen = (row == index).astype(jnp.bfloat16)
    return lax.dot_general(
        chosen, ancestor, (((0,), (0,)), ((), ())), preferred_element_type=jnp.float32
    ).astype(jnp.bfloat16)


def pick_shares_kernel(
    counts_hbm, lists_hbm, ancestor_hbm, kept_ref, sent_ref, live_ref, held_ref, counts_ref, sems
):
    copies = [
        pltpu.make_async_copy(source, target, sems.at[i])
        for i, (source, target) in enumerate(
            ((counts_hbm, counts_ref), (lists_hbm.at[0], live_ref), (ancestor_hbm, held_ref))
        )
    ]
    for copy in copies:
        copy.start()
    for copy in copies[:2]:
        copy.wait()
    slot_rows = live_ref.shape[-1]
    share = slot_rows // lax.axis_size("row")
    first = lax.axis_index("row") * share
    chip, core = place()
    lane = lax.broadcasted_iota(jnp.int32, (1, 2 * share), 1)
    slot = lax.broadcasted_iota(jnp.int32, (1, slot_rows), 1)
    for d in range(live_ref.shape[0]):
        live_ref[d] = jnp.where(slot < counts_ref[d], live_ref[d], -1)

    def rolled(d, start):
        row = jnp.broadcast_to(live_ref[d], (8, slot_rows))
        return pltpu.roll(row, lax.rem(slot_rows - first + start, slot_rows), 1)[:1, : 2 * share]

    chosen = []
    for step in FAR:
        kept = rolled(2 * moved(chip, step, core, 1) + core, 0)
        sent = rolled(2 * moved(chip, step, 1 - core, 1) + 1 - core, share)
        chosen.append(jnp.where(lane < share, kept, sent))
    copies[2].wait()
    for i, index in enumerate(chosen):
        rows = picked_rows(held_ref[...], index)
        kept_ref[i] = rows[:share]
        sent_ref[i] = rows[share:]


def pick_slots_kernel(steps, live_ref, held_ref, kept_ref, sent_ref):
    chip, core = place()
    ancestor = held_ref[...]
    for i, step in enumerate(steps):
        for to, ref in ((1 - core, sent_ref), (core, kept_ref)):
            ref[i] = picked_rows(ancestor, live_ref[2 * moved(chip, step, to, 1) + to])


def pick_shares(counts, lists, ancestor):
    share = lists.shape[-1] // lax.axis_size("row")
    vmem = pl.BlockSpec(memory_space=pltpu.VMEM)
    shape = jax.ShapeDtypeStruct((len(FAR), share, ancestor.shape[1]), ancestor.dtype)
    return pl.pallas_call(
        pick_shares_kernel,
        out_shape=(
            shape,
            shape,
            jax.ShapeDtypeStruct(lists.shape[1:], lists.dtype),
            jax.ShapeDtypeStruct(ancestor.shape, ancestor.dtype),
        ),
        in_specs=[pl.BlockSpec(memory_space=pltpu.HBM)] * 3,
        out_specs=(vmem,) * 4,
        scratch_shapes=[
            pltpu.SMEM(counts.shape, counts.dtype),
            pltpu.SemaphoreType.DMA((3,)),
        ],
        compiler_params=pltpu.CompilerParams(vmem_limit_bytes=24 << 20),
    )(*(pltpu.with_memory_space_constraint(x, pltpu.HBM) for x in (counts, lists, ancestor)))


def pick_slots(steps, lists, ancestor):
    vmem = pl.BlockSpec(memory_space=pltpu.VMEM)
    rows = lists.shape[-1]
    shape = jax.ShapeDtypeStruct((len(steps), rows, ancestor.shape[1]), ancestor.dtype)
    return pl.pallas_call(
        functools.partial(pick_slots_kernel, steps),
        out_shape=(shape, shape),
        in_specs=[vmem, vmem],
        out_specs=(vmem, vmem),
        compiler_params=pltpu.CompilerParams(vmem_limit_bytes=24 << 20),
        cost_estimate=pl.CostEstimate(
            flops=4 * len(steps) * rows * ancestor.size,
            bytes_accessed=2 * ancestor.size,
            transcendentals=0,
        ),
    )(lists, ancestor)


def columns(coeff_ref, chip, top, height):
    width = coeff_ref.shape[1] // CHIPS
    return coeff_ref[top : top + height, pl.ds(pl.multiple_of(chip * width, width), width)]


def near_kernel(coeff_ref, kept_ref, came_ref, *refs):
    *part_refs, sum_ref, rows_ref = refs
    chip, core = place()
    slot_rows = kept_ref.shape[0]
    kept, came = kept_ref[...], came_ref[...]
    rows_ref[0, :slot_rows] = jnp.where(core == 0, kept, came)
    rows_ref[0, slot_rows:] = jnp.where(core == 0, came, kept)
    pivots = coeff_ref.shape[0]
    sum_ref[...] = jnp.dot(
        columns(coeff_ref, chip, 0, pivots), rows_ref[0], preferred_element_type=jnp.float32
    )
    for i, (step, part_ref) in enumerate(zip(MID + NEAR[:2], part_refs, strict=True), 1):
        for holder in range(2):
            rows_ref[i, holder * slot_rows : (holder + 1) * slot_rows] = part_ref[
                lax.bitwise_xor(core, holder)
            ]
        sum_ref[...] += jnp.dot(
            columns(coeff_ref, moved(chip, step, core, -1), 0, pivots),
            rows_ref[i],
            preferred_element_type=jnp.float32,
        )


def far_kernel(
    part, coeff_ref, sum_ref, own_ref, across_ref, before_ref, after_ref, out_ref, rows_ref
):
    chip, core = place()
    me = lax.axis_index("row")
    peers = lax.axis_size("row")
    share = own_ref.shape[2]
    half = out_ref.shape[0]
    total = sum_ref[part * half : (part + 1) * half]
    for i, step in enumerate(FAR):
        for block in range(peers):
            back = lax.rem(block - me + peers, peers)
            for holder in range(2):
                piece = before_ref[i, lax.bitwise_xor(core, holder)]
                for away, part_ref in ((2, across_ref), (1, after_ref), (0, own_ref)):
                    piece = jnp.where(
                        back == away, part_ref[i, lax.bitwise_xor(core, holder)], piece
                    )
                start = (holder * peers + block) * share
                rows_ref[i, start : start + share, :] = piece
        total = total + jnp.dot(
            columns(coeff_ref, moved(chip, step, core, -1), part * half, half),
            rows_ref[i],
            preferred_element_type=jnp.float32,
        )
    out_ref[...] = total.astype(out_ref.dtype)


def products(coeff, kept, came, mid, near, shares):
    vmem = pl.BlockSpec(memory_space=pltpu.VMEM)
    pivots, sources = coeff.shape[0], kept.shape[-1]
    depth = coeff.shape[1] // CHIPS

    def cost(blocks):
        return pl.CostEstimate(
            flops=int(2 * blocks) * depth * pivots * sources,
            bytes_accessed=int(2 * blocks) * depth * (pivots + sources),
            transcendentals=0,
        )

    total = pl.pallas_call(
        near_kernel,
        out_shape=jax.ShapeDtypeStruct((pivots, sources), jnp.float32),
        in_specs=[vmem] * (len(MID + NEAR) + 2),
        out_specs=vmem,
        scratch_shapes=[pltpu.VMEM((len(MID + NEAR), depth, sources), coeff.dtype)],
        compiler_params=pltpu.CompilerParams(vmem_limit_bytes=24 << 20),
        cost_estimate=cost(len(MID + NEAR)),
    )(coeff, kept, came, *mid, *near)
    half = jax.ShapeDtypeStruct((pivots // 2, sources), coeff.dtype)
    return [
        pl.pallas_call(
            functools.partial(far_kernel, part),
            out_shape=half,
            in_specs=[vmem] * 6,
            out_specs=vmem,
            scratch_shapes=[pltpu.VMEM((len(FAR), depth, sources), coeff.dtype)],
            compiler_params=pltpu.CompilerParams(vmem_limit_bytes=24 << 20),
            cost_estimate=cost(len(FAR) / 2),
        )(coeff, total, *shares)
        for part in range(2)
    ]


def added(a, b):
    return (a.astype(jnp.float32) + b.astype(jnp.float32)).astype(jnp.bfloat16)


def per_device(ancestor, send_rows, send_count, border_coeff, right_side, pivot_inverse):
    kept, sent, live, held = pick_shares(send_count.reshape(-1), send_rows, ancestor)
    came = even_swap(sent, "front")
    far = jnp.stack([kept, came], 1)
    kept, sent = pick_slots(NEAR, live, held)
    came = even_swap(sent, "front")
    near = jnp.stack([kept, came], 1)
    kept, sent = pick_slots(MID, live, held)
    came = even_swap(sent, "front")
    mid = jnp.stack([kept, came], 1)
    sent = []
    for part, steps in ((near, NEAR[:2]), (far, FAR), (mid, MID)):
        for i, step in enumerate(steps):
            sent.append(along_chips(part[i], step))
    near_parts, mid_parts = sent[:2], sent[2 + len(FAR) :]
    shares = [jnp.stack(sent[2 : 2 + len(FAR)])]
    for step in (2, 1, -1):
        shares.append(shifted(shares[0], "row", step))
    coeff = pltpu.with_memory_space_constraint(border_coeff[0], pltpu.VMEM)
    rhs = right_side[0]
    inverse = pivot_inverse[0]
    half = coeff.shape[0] // 2
    halves = products(coeff, near[2, 0], near[2, 1], mid_parts, near_parts, shares)
    parts = []
    for i, (one, two) in enumerate(((even_swap, odd_swap), (odd_swap, even_swap))):
        rows = slice(i * half, (i + 1) * half)
        pair = added(halves[i], one(halves[i], "col"))
        other = two(pair, "col")
        total = pair.astype(jnp.float32) + other.astype(jnp.float32)
        parts.append((rhs[rows].astype(jnp.float32) - total).astype(jnp.bfloat16))
    residual = jnp.concatenate(parts, 0)
    term = lax.dot_general(
        residual, inverse, (((0,), (0,)), ((), ())), preferred_element_type=jnp.float32
    ).astype(jnp.bfloat16)
    peers = lax.axis_size("row")
    tiles = term.reshape(peers, term.shape[0] // peers, term.shape[1])
    me = lax.axis_index("row")

    def tile(step):
        return lax.dynamic_index_in_dim(tiles, lax.rem(me + step, peers), 0, keepdims=False)

    answer = tile(0).astype(jnp.float32)
    for step in (2, 1, 3):
        answer = answer + shifted(tile(step), "row", step).astype(jnp.float32)
    return answer[None]


def solution(mesh):
    return sharded(per_device, mesh)


def sharded(body, mesh):
    return jax.shard_map(
        body,
        mesh=mesh,
        in_specs=(
            P("front", None),
            P("front", None, "col", None),
            P("front", None, "col"),
            P("front", "row", "col"),
            P("front", "row", None),
            P("front", "row", "col"),
        ),
        out_specs=P("front", "row", "col"),
        check_vma=False,
    )
```
